32 devices in a mesh: shots: 2 (over y), depth: 4 (over z), row: 4 (over x, core).
Axes of the slice: x: 2, y: 2, z: 4, core: 2. Of those that a mesh axis runs over, the one named last changes fastest.
Arguments:
- waves: float32 [8, 2, 512, 2, 1, 512], P(('shots', 'depth'), None, 'row'), parts along dimension 0, may hold values from -6 to 6
- slab_freq: float32 [8, 1], P(('shots', 'depth')), parts along dimension 0, may hold values from 1.2 to 2.4
- slowness: float32 [4, 512, 512], P('depth', 'row'), may hold values from 0.8 to 1.25
- ref_slow: float32 [4], P('depth'), may hold values from 0.9 to 1.1
- inj_freq: float32 [2, 1], P('shots'), parts along dimension 0, may hold values from 1.2 to 2.4
- wavelet: float32 [2, 1, 2], P('shots'), parts along dimension 0, may hold values from -64 to 64
- records: float32 [2, 1, 2, 4096], P('shots'), parts along dimension 0, may hold values from -6 to 6
- src_pos: int32 [4], P('shots'), parts along dimension 0, may hold values from 0 to 511
- rcv_pos: int32 [8192, 2], P('shots'), parts along dimension 0, may hold values from 0 to 511
Outputs:
- wave_out: float32 [8, 2, 512, 2, 1, 512], P(('shots', 'depth'), None, 'row'), parts along dimension 0
- image: float32 [8, 16, 512, 512], P(('shots', 'depth'), None, 'row'), parts along dimension 0
The draws below stay inside these ranges and needn't reach their ends.
There are 2 independent parts, one for each index of `shots`. The reference program is written for one: setup_inputs(seed, part) draws one part's arguments, and reference() takes and returns one part's arrays. A program takes and returns all parts, laid end to end along the dimension named above; an argument that names none is the same for every part. Nothing has to cross between parts.
All inputs are finite; a program needn't handle non-finite values.
Results may differ from the reference program's by a relative error of at most 0.0003.
Values sent between devices are 32-bit elements; how exact they have to be, the bound alone decides.
A program may use at most 128 MiB of HBM per device.

```python
import math
import jax
import jax.numpy as jnp
from jax import lax

NL = 512
OFF = 16
F = 1
PLANES_DEV = 1
TICKS = 2
NREC = 4096
DZ = 4
GROUPS = 4
DEPTHS = 4


def place_ends(entries, key, smallest, top_value):
    extent = entries.shape
    spot = [jax.random.randint(jax.random.fold_in(key, axis), (), 0, extent[axis]) for axis in range(len(extent))]
    entries = entries.at[tuple(spot)].set(smallest)
    longest = extent.index(max(extent))
    spot[longest] = (spot[longest] + 1) % extent[longest]
    return entries.at[tuple(spot)].set(top_value)


def block_levels(rng, extent, split, least, largest):
    factor_of = 1.0
    for position, shards_of in split:
        steps = jax.random.uniform(jax.random.fold_in(jax.random.fold_in(rng, 6), position), (shards_of,), jnp.float32, least / len(split), largest / len(split))
        factor_of = factor_of * jnp.repeat(jnp.exp(steps), extent[position] // shards_of).reshape((-1,) + (1,) * (len(extent) - 1 - position))
    return factor_of


def scatter_about(stream_key, shape, width, most, pieces=(), kind=jnp.bfloat16):
    values = width * jax.random.normal(stream_key, shape, jnp.float32)
    if pieces:
        values = values * block_levels(stream_key, shape, pieces, -0.22, 0.18)
    return jnp.clip(values, -most, most).astype(kind)


def setup_inputs(seed: int = 0, part: int = 0) -> dict:
    seeds = jax.random.split(jax.random.key(seed), 10)
    own_keys = jax.random.split(jax.random.fold_in(seeds[9], part), 10)
    return {
        "waves": scatter_about(own_keys[0], (GROUPS, 2, NL, 2, F, NL), 1.0, 6.0, ((0, 4), (2, 4)), jnp.float32),
        "slab_freq": jnp.clip(1.2 + 1.2 * jax.random.uniform(own_keys[1], (GROUPS, F), jnp.float32) ** block_levels(own_keys[1], (GROUPS, F), ((0, 4),), -0.2, 0.2), 1.2, 2.4),
        "slowness": jnp.clip(jnp.exp(math.log(1.25) - 0.4462871 * jax.random.uniform(seeds[2], (DEPTHS, NL, NL), jnp.float32) ** block_levels(seeds[2], (DEPTHS, NL, NL), ((0, 4), (1, 4)), -0.2, 0.2)), 0.8, 1.25),
        "ref_slow": jnp.clip(0.9 + 0.20000005 * jax.random.uniform(seeds[3], (DEPTHS,), jnp.float32) ** block_levels(seeds[3], (DEPTHS,), ((0, 4),), -0.2, 0.2), 0.9, 1.1),
        "inj_freq": jnp.clip(jax.random.uniform(own_keys[4], (TICKS - 1, F), jnp.float32, 1.2, 2.4), 1.2, 2.4),
        "wavelet": scatter_about(own_keys[5], (TICKS - 1, F, 2), 16.0, 64.0, (), jnp.float32),
        "records": scatter_about(own_keys[6], (TICKS - 1, F, 2, NREC), 1.0, 6.0, (), jnp.float32),
        "src_pos": jax.random.randint(own_keys[7], (2,), 0, NL).astype(jnp.int32),
        "rcv_pos": place_ends(jax.random.randint(own_keys[8], (NREC, 2), 0, NL), jax.random.fold_in(own_keys[8], 1), 0, NL - 1).astype(jnp.int32),
    }


def inject(tick_now, wavelet, records, src_pos, rcv_pos):
    lateral_cells = jnp.arange(NL, dtype=jnp.int32)
    source_point = ((lateral_cells == src_pos[0])[:, None] & (lateral_cells == src_pos[1])[None, :]).astype(jnp.float32)
    amplitude = wavelet[tick_now, :, 0] + 1j * wavelet[tick_now, :, 1]
    source = amplitude[:, None, None] * source_point[None]
    recorded = records[tick_now, :, 0] + 1j * records[tick_now, :, 1]
    receiver = jnp.zeros((F, NL, NL), recorded.dtype).at[:, rcv_pos[:, 0], rcv_pos[:, 1]].add(recorded)
    return jnp.stack([source, receiver])

def reference(waves, slab_freq, slowness, ref_slow, inj_freq, wavelet, records, src_pos, rcv_pos):
    half_width = OFF // 2
    wave_field = waves[:, 0] + 1j * waves[:, 1]
    wave_field = jnp.transpose(wave_field, (0, 2, 3, 1, 4))
    field_signs = jnp.array([1.0, -1.0], jnp.float32)[None, :, None, None, None]
    wave_numbers = jnp.fft.fftfreq(NL) * (2.0 * math.pi)
    wave_sq = wave_numbers[:, None] ** 2 + wave_numbers[None, :] ** 2
    freq_now = slab_freq
    slow_planes = slowness.reshape(GROUPS, PLANES_DEV, NL, NL)
    ref_planes = ref_slow.reshape(GROUPS, PLANES_DEV)
    image_sum = jnp.zeros((GROUPS, PLANES_DEV, OFF, NL, NL), jnp.float32)
    for tick_now in range(TICKS):
        for plane_index in range(PLANES_DEV):
            ref_number = freq_now * ref_planes[:, plane_index][:, None]
            vertical_sq = (ref_number * ref_number)[:, :, None, None] - wave_sq
            root_abs = jnp.sqrt(jnp.abs(vertical_sq))
            propagating = vertical_sq > 0
            phase_real = jnp.where(propagating, jnp.cos(root_abs * DZ), jnp.exp(-root_abs * DZ))
            phase_imag = jnp.where(propagating, jnp.sin(root_abs * DZ), 0.0)
            phase_shift = phase_real[:, None] + 1j * field_signs * phase_imag[:, None]
            wave_field = jnp.fft.ifft2(jnp.fft.fft2(wave_field) * phase_shift)
            contrast = slow_planes[:, plane_index] - ref_planes[:, plane_index][:, None, None]
            lens_angle = field_signs * freq_now[:, None, :, None, None] * contrast[:, None, None] * DZ
            wave_field = wave_field * (jnp.cos(lens_angle) + 1j * jnp.sin(lens_angle))
            padded = jnp.pad(wave_field, ((0, 0), (0, 0), (0, 0), (half_width, half_width), (0, 0)))
            offset_terms = []
            for offset_index in range(OFF):
                offset_lag = offset_index - half_width
                source = padded[:, 0, :, half_width - offset_lag:half_width - offset_lag + NL]
                receiver = padded[:, 1, :, half_width + offset_lag:half_width + offset_lag + NL]
                product = jnp.real(source) * jnp.real(receiver) + jnp.imag(source) * jnp.imag(receiver)
                offset_terms.append(lax.optimization_barrier(jnp.sum(product, axis=1)))
            image_sum = image_sum.at[:, plane_index].add(jnp.stack(offset_terms, axis=1))
        if tick_now + 1 < TICKS:
            injected = inject(tick_now, wavelet, records, src_pos, rcv_pos)
            wave_field = jnp.concatenate([injected[None], wave_field[:-1]], axis=0)
            freq_now = jnp.concatenate([inj_freq[tick_now][None], freq_now[:-1]], axis=0)
    wave_field = jnp.transpose(wave_field, (0, 3, 1, 2, 4))
    wave_out = jnp.stack([jnp.real(wave_field), jnp.imag(wave_field)], axis=1).astype(jnp.float32)
    image = image_sum.reshape(GROUPS * PLANES_DEV, OFF, NL, NL).astype(jnp.float32)
    return (wave_out, image)
```

```python
import functools
import math

import jax
import jax.numpy as jnp
import numpy as np
from jax import lax
from jax.experimental import pallas as pl
from jax.experimental.pallas import tpu as pltpu
from jax.sharding import PartitionSpec as P

OFF = 16
TICKS = 2
DZ = 4

MESH = pl.DeviceIdType.MESH
NT = (((1,), (1,)), ((), ()))
NN = (((1,), (0,)), ((), ()))


def half_tables(length):
    half = length // 2
    a = np.arange(half)
    mats = []
    for odd in (0, 1):
        turn = ((2 * a[:, None] + odd) * a[None, :]) % length
        angle = turn * (2.0 * math.pi / length)
        c, s = np.cos(angle), np.sin(angle)
        mats.append(np.block([[c, s], [-s, c]]))
    stacked = []
    for m in (mats[0], mats[1]):
        high = m.astype(np.float32).astype(jnp.bfloat16)
        low = (m - high.astype(np.float64)).astype(np.float32).astype(jnp.bfloat16)
        stacked += [high, low]
    return np.stack(stacked)


def split(value):
    high = value.astype(jnp.bfloat16)
    low = (value - high.astype(jnp.float32)).astype(jnp.bfloat16)
    return high, low


def dot(a, b, dims):
    return lax.dot_general(a, b, dims, preferred_element_type=jnp.float32)


def table_first(high, low, data):
    d_high, d_low = split(data)
    return dot(high, d_high, NT) + (dot(high, d_low, NT) + dot(low, d_high, NT))


def data_first(data, high, low):
    d_high, d_low = split(data)
    return dot(d_high, high, NN) + (dot(d_low, high, NN) + dot(d_high, low, NN))


def cos_sin(angle):
    turns = jnp.floor(angle * (2.0 / math.pi) + 0.5)
    r = angle - turns * 1.5703125
    r = r - turns * 4.837512969970703125e-4
    r = r - turns * 7.54978995489188216e-8
    z = r * r
    sine = r + r * z * (-1.6666654611e-1 + z * (8.3321608736e-3 + z * -1.9515295891e-4))
    cosine = 1.0 - 0.5 * z + z * z * (
        4.166664568298827e-2 + z * (-1.388731625493765e-3 + z * 2.443315711809948e-5)
    )
    quarter = turns.astype(jnp.int32)
    swap = (quarter & 1) == 1
    c = jnp.where(swap, sine, cosine)
    s = jnp.where(swap, cosine, sine)
    c = jnp.where(((quarter + 1) & 2) == 2, -c, c)
    s = jnp.where((quarter & 2) == 2, -s, s)
    return c, s


def kernel(
    n, depths, rows, cols, length, nrec,
    freq_ref, slow_ref, inj_ref, wavelet_ref, src_ref,
    waves_ref, table_ref, slowness_ref, pos_ref, rec_ref,
    shown_ref, image_out,
    u_first, image_ref, table_t, u_next, send1, recv1, send2, recv2, fld, phase, lens, freq_out, freq_in, hot,
    a2a_send, a2a_recv, z_send, z_recv, halo_send, halo_recv, f_send, f_recv, w_sem, i_sem, o_sem,
):
    half = length // 2
    wide = OFF // 2
    me = lax.axis_index("row")
    level = lax.axis_index("depth")
    deeper = level < depths - 1
    has_above = level > 0
    has_prev = me > 0
    has_next = me < n - 1

    def peer(off):
        return lax.rem(me + off, n)

    order = sorted(range(1, n), key=lambda off: abs(off - n / 2))

    def wave_copy(p, f):
        return pltpu.make_async_copy(waves_ref.at[p, :, f, 0, :], u_first.at[p, f], w_sem.at[p, f])

    def image_copy():
        return pltpu.make_async_copy(image_ref, image_out, i_sem)

    def shown_copy(f):
        return pltpu.make_async_copy(fld.at[TICKS - 1, :, f], shown_ref.at[:, f], o_sem.at[f])

    for f in (0, 1):
        for p in (0, 1):
            wave_copy(p, f).start()

    freq_out[...] = jnp.full(freq_out.shape, freq_ref[0, 0], jnp.float32)
    barrier = pltpu.get_barrier_semaphore()
    for off in order:
        pl.semaphore_signal(barrier, inc=1, device_id={"row": peer(off)}, device_id_type=MESH)

    @pl.when(deeper)
    def _():
        pl.semaphore_signal(barrier, inc=1, device_id={"depth": level + 1}, device_id_type=MESH)

    @pl.when(has_above)
    def _():
        pl.semaphore_signal(barrier, inc=1, device_id={"depth": level - 1}, device_id_type=MESH)

    sides = jnp.where(deeper, 1, 0) + jnp.where(has_above, 1, 0)
    pl.semaphore_wait(barrier, n - 1 + sides)

    below = lax.rem(level + 1, depths)

    def freq_copy():
        return pltpu.make_async_remote_copy(
            src_ref=freq_out, dst_ref=freq_in, send_sem=f_send, recv_sem=f_recv,
            device_id={"depth": below}, device_id_type=MESH)

    def z_copy(f):
        return pltpu.make_async_remote_copy(
            src_ref=fld.at[0, :, f, pl.ds(wide, rows), :], dst_ref=u_next.at[:, f],
            send_sem=z_send.at[f], recv_sem=z_recv.at[f],
            device_id={"depth": below}, device_id_type=MESH)

    def a2a1_copy(t, f, off):
        to = peer(off)
        return pltpu.make_async_remote_copy(
            src_ref=send1.at[t, f, pl.ds(pl.multiple_of(to * cols, cols), cols), :],
            dst_ref=recv1.at[t, f, me],
            send_sem=a2a_send.at[t, 0, f, off], recv_sem=a2a_recv.at[t, 0, f, off],
            device_id={"row": to}, device_id_type=MESH)

    def a2a2_copy(t, f, off):
        to = peer(off)
        return pltpu.make_async_remote_copy(
            src_ref=send2.at[t, f, pl.ds(pl.multiple_of(to * rows, rows), rows), :],
            dst_ref=recv2.at[t, f, me],
            send_sem=a2a_send.at[t, 1, f, off], recv_sem=a2a_recv.at[t, 1, f, off],
            device_id={"row": to}, device_id_type=MESH)

    def up_copy(t):
        return pltpu.make_async_remote_copy(
            src_ref=fld.at[t, :, :, pl.ds(rows, wide), :], dst_ref=fld.at[t, :, :, pl.ds(0, wide), :],
            send_sem=halo_send.at[t, 0], recv_sem=halo_recv.at[t, 0],
            device_id={"row": peer(1)}, device_id_type=MESH)

    def down_copy(t):
        return pltpu.make_async_remote_copy(
            src_ref=fld.at[t, :, :, pl.ds(wide, wide), :],
            dst_ref=fld.at[t, :, :, pl.ds(rows + wide, wide), :],
            send_sem=halo_send.at[t, 1], recv_sem=halo_recv.at[t, 1],
            device_id={"row": peer(n - 1)}, device_id_type=MESH)

    @pl.when(deeper)
    def _():
        freq_copy().start()

    def forward_y(t, f, real, imag):
        for parity in (0, 1):
            if parity == 0:
                folded = jnp.concatenate(
                    [real[:, :half] + real[:, half:], imag[:, :half] + imag[:, half:]], axis=1)
            else:
                folded = jnp.concatenate(
                    [real[:, :half] - real[:, half:], imag[:, :half] - imag[:, half:]], axis=1)
            result = table_first(table_ref[2 * parity], table_ref[2 * parity + 1], folded)
            send1[t, f, pl.ds(parity * half, half), pl.ds(0, rows)] = result[:half]
            send1[t, f, pl.ds(parity * half, half), pl.ds(rows, rows)] = result[half:]
        for off in order:
            a2a1_copy(t, f, off).start()
        recv1[t, f, me] = send1[t, f, pl.ds(pl.multiple_of(me * cols, cols), cols), :]

    def middle(t, f):
        for off in order:
            a2a1_copy(t, f, off).wait_recv()
        sign = 1.0 if f == 0 else -1.0
        real = jnp.concatenate([recv1[t, f, s, :, pl.ds(0, rows)] for s in range(n)], axis=1)
        imag = jnp.concatenate([recv1[t, f, s, :, pl.ds(rows, rows)] for s in range(n)], axis=1)
        results = []
        for parity in (0, 1):
            if parity == 0:
                folded = jnp.concatenate(
                    [real[:, :half] + real[:, half:], imag[:, :half] + imag[:, half:]], axis=1)
            else:
                folded = jnp.concatenate(
                    [real[:, :half] - real[:, half:], imag[:, :half] - imag[:, half:]], axis=1)
            spectrum = data_first(folded, table_t[2 * parity], table_t[2 * parity + 1])
            p_real = phase[t, 0, :, pl.ds(parity * half, half)]
            p_imag = phase[t, 1, :, pl.ds(parity * half, half)] * sign
            s_real, s_imag = spectrum[:, :half], spectrum[:, half:]
            shifted = jnp.concatenate(
                [s_real * p_real - s_imag * p_imag, s_real * p_imag + s_imag * p_real], axis=1)
            results.append(table_first(table_t[2 * parity], table_t[2 * parity + 1], shifted))
        total = results[0] + results[1]
        send2[t, f, pl.ds(0, half), pl.ds(0, cols)] = total[:half]
        send2[t, f, pl.ds(0, half), pl.ds(cols, cols)] = total[half:]
        total = results[0] - results[1]
        send2[t, f, pl.ds(half, half), pl.ds(0, cols)] = total[:half]
        send2[t, f, pl.ds(half, half), pl.ds(cols, cols)] = total[half:]
        for off in order:
            a2a2_copy(t, f, off).start()
        recv2[t, f, me] = send2[t, f, pl.ds(pl.multiple_of(me * rows, rows), rows), :]

    def inverse_y(t, f):
        for off in order:
            a2a2_copy(t, f, off).wait_recv()
        sign = 1.0 if f == 0 else -1.0
        real = jnp.concatenate([recv2[t, f, s, :, pl.ds(0, cols)] for s in range(n)], axis=1)
        imag = jnp.concatenate([recv2[t, f, s, :, pl.ds(cols, cols)] for s in range(n)], axis=1)
        even = data_first(
            jnp.concatenate([real[:, :half], imag[:, :half]], axis=1), table_ref[0], table_ref[1])
        odd = data_first(
            jnp.concatenate([real[:, half:], imag[:, half:]], axis=1), table_ref[2], table_ref[3])
        for part in (0, 1):
            total = even + odd if part == 0 else even - odd
            window = pl.ds(part * half, half)
            l_cos = lens[t, 0, :, window]
            l_sin = lens[t, 1, :, window] * sign
            t_real, t_imag = total[:, :half], total[:, half:]
            fld[t, 0, f, pl.ds(wide, rows), window] = t_real * l_cos - t_imag * l_sin
            fld[t, 1, f, pl.ds(wide, rows), window] = t_real * l_sin + t_imag * l_cos

    def wave_number(index):
        order_of = jnp.where(index < half, 2 * index, 2 * (index - half) + 1)
        signed = jnp.where(order_of < half, order_of, order_of - length)
        k = signed.astype(jnp.float32) * (2.0 * math.pi / length)
        return k * k

    def factors(t, freq):
        ref_slow = slow_ref[0]
        number = freq * ref_slow
        block = min(cols, 32)

        def phase_block(i, carry):
            base = pl.multiple_of(i * block, block)
            ky = wave_number(lax.broadcasted_iota(jnp.int32, (block, length), 0) + (me * cols + base))
            kx = wave_number(lax.broadcasted_iota(jnp.int32, (block, length), 1))
            vertical = number * number - (kx + ky)
            root = jnp.sqrt(jnp.abs(vertical)) * float(DZ)
            moving = vertical > 0
            c, s = cos_sin(root)
            scale = 1.0 / (length * length)
            phase[t, 0, pl.ds(base, block), :] = jnp.where(moving, c, jnp.exp(-root)) * scale
            phase[t, 1, pl.ds(base, block), :] = jnp.where(moving, s, 0.0) * scale
            return carry

        lax.fori_loop(0, cols // block, phase_block, 0)
        block_r = min(rows, 32)

        def lens_block(i, carry):
            base = pl.multiple_of(i * block_r, block_r)
            angle = freq * (slowness_ref[pl.ds(base, block_r), :] - ref_slow) * float(DZ)
            c, s = cos_sin(angle)
            lens[t, 0, pl.ds(base, block_r), :] = c
            lens[t, 1, pl.ds(base, block_r), :] = s
            return carry

        lax.fori_loop(0, rows // block_r, lens_block, 0)

    def inject():
        row_ids = lax.broadcasted_iota(jnp.int32, (rows, 1), 0) + me * rows
        col_ids = lax.broadcasted_iota(jnp.int32, (1, length), 1)
        point = (row_ids == src_ref[0]) & (col_ids == src_ref[1])
        for p in (0, 1):
            u_next[p, 0] = jnp.where(point, wavelet_ref[0, p], 0.0)
        chunk = min(512, nrec)

        def step(i, carry):
            base = pl.multiple_of(i * chunk, chunk)
            x = pos_ref[pl.ds(0, 1), pl.ds(base, chunk)]
            y = pos_ref[pl.ds(1, 1), pl.ds(base, chunk)]
            in_row = lax.broadcasted_iota(jnp.int32, (rows, chunk), 0) + me * rows == x
            in_col = jnp.where(
                lax.broadcasted_iota(jnp.int32, (length, chunk), 0) == y, 1.0, 0.0).astype(jnp.bfloat16)
            parts = []
            for p in (0, 1):
                value = rec_ref[pl.ds(p, 1), pl.ds(base, chunk)]
                parts.append(jnp.where(in_row, value, 0.0))
            left = jnp.concatenate(parts, axis=0)
            high, low = split(left)
            added = dot(high, in_col, NT) + dot(low, in_col, NT)
            hot[...] = hot[...] + added
            return carry

        hot[...] = jnp.zeros_like(hot)
        lax.fori_loop(0, nrec // chunk, step, 0)
        u_next[0, 1] = hot[pl.ds(0, rows), :]
        u_next[1, 1] = hot[pl.ds(rows, rows), :]

    def halo_start(t):
        zero = jnp.zeros((2, 2, wide, length), jnp.float32)

        @pl.when(has_next)
        def _():
            up_copy(t).start()

        @pl.when(has_prev)
        def _():
            down_copy(t).start()

        @pl.when(jnp.logical_not(has_prev))
        def _():
            fld[t, :, :, pl.ds(0, wide), :] = zero

        @pl.when(jnp.logical_not(has_next))
        def _():
            fld[t, :, :, pl.ds(rows + wide, wide), :] = zero

    def halo_wait(t):
        @pl.when(has_prev)
        def _():
            up_copy(t).wait_recv()

        @pl.when(has_next)
        def _():
            down_copy(t).wait_recv()

    def imaging(t):
        def block(i, carry):
            base = pl.multiple_of(i * 8, 8)
            window = pl.ds(base, 8 + 2 * wide)
            values = [fld[t, p, f, window, :] for f in (0, 1) for p in (0, 1)]
            for j in range(OFF):
                h = j - wide
                s_real, s_imag = (v[wide - h:wide - h + 8] for v in values[:2])
                r_real, r_imag = (v[wide + h:wide + h + 8] for v in values[2:])
                term = s_real * r_real + s_imag * r_imag
                image_ref[j, pl.ds(base, 8), :] = term
            return carry

        lax.fori_loop(0, rows // 8, block, 0)

    for f in (0, 1):
        for p in (0, 1):
            wave_copy(p, f).wait()
        forward_y(0, f, u_first[0, f], u_first[1, f])
    for i in range(4):
        table_t[i] = table_ref[i].T
    factors(0, freq_ref[0, 0])
    for f in (0, 1):
        middle(0, f)

    @pl.when(jnp.logical_not(has_above))
    def _():
        factors(1, inj_ref[0, 0])

    @pl.when(has_above)
    def _():
        freq_copy().wait_recv()
        factors(1, freq_in[pl.ds(0, 1), pl.ds(0, 1)])

    for f in (0, 1):
        inverse_y(0, f)

        @pl.when(deeper)
        def _():
            z_copy(f).start()

    halo_start(0)

    @pl.when(jnp.logical_not(has_above))
    def _():
        inject()

    halo_wait(0)
    imaging(0)
    image_copy().start()

    for f in (0, 1):
        @pl.when(has_above)
        def _():
            z_copy(f).wait_recv()

        forward_y(1, f, u_next[0, f], u_next[1, f])
    for f in (0, 1):
        middle(1, f)
    for f in (0, 1):
        inverse_y(1, f)
    halo_start(1)
    halo_wait(1)
    for f in (0, 1):
        shown_copy(f).start()
    for t in range(TICKS):
        for f in (0, 1):
            for off in order:
                a2a1_copy(t, f, off).wait_send()
                a2a2_copy(t, f, off).wait_send()

        @pl.when(has_next)
        def _():
            up_copy(t).wait_send()

        @pl.when(has_prev)
        def _():
            down_copy(t).wait_send()

    @pl.when(deeper)
    def _():
        freq_copy().wait_send()
        for f in (0, 1):
            z_copy(f).wait_send()

    image_copy().wait()
    for f in (0, 1):
        shown_copy(f).wait()


def finish(rows, length, fld_ref, before_ref, out_ref, image_ref, o_sem):
    wide = OFF // 2
    step = pl.program_id(0)
    block = image_ref.shape[1]

    def out_copy(p, f):
        return pltpu.make_async_copy(
            fld_ref.at[p, f, pl.ds(wide, rows), :], out_ref.at[p, :, f, 0, :], o_sem.at[p, f])

    @pl.when(step == 0)
    def _():
        for f in (0, 1):
            for p in (0, 1):
                out_copy(p, f).start()

    def part(i, carry):
        base = pl.multiple_of(i * 8, 8)
        window = pl.ds(pl.multiple_of(step * block + base, 8), 8 + 2 * wide)
        values = [fld_ref[p, f, window, :] for f in (0, 1) for p in (0, 1)]
        for j in range(OFF):
            h = j - wide
            s_real, s_imag = (v[wide - h:wide - h + 8] for v in values[:2])
            r_real, r_imag = (v[wide + h:wide + h + 8] for v in values[2:])
            term = s_real * r_real + s_imag * r_imag
            image_ref[j, pl.ds(base, 8), :] = before_ref[j, pl.ds(base, 8), :] + term
        return carry

    lax.fori_loop(0, block // 8, part, 0)

    @pl.when(step == pl.num_programs(0) - 1)
    def _():
        for f in (0, 1):
            for p in (0, 1):
                out_copy(p, f).wait()


def solution(mesh):
    n, depths = mesh.shape["row"], mesh.shape["depth"]

    def local(waves, slab_freq, slowness, ref_slow, inj_freq, wavelet, records, src_pos, rcv_pos):
        rows, length = waves.shape[2], waves.shape[5]
        cols = length // n
        nrec = rcv_pos.shape[0]
        assert waves.shape[4] == 1 and slowness.shape[0] == 1
        assert inj_freq.shape[0] == TICKS - 1
        table = jnp.asarray(half_tables(length), jnp.bfloat16)
        vmem = pl.BlockSpec(memory_space=pltpu.VMEM)
        smem = pl.BlockSpec(memory_space=pltpu.SMEM)
        f32 = jnp.float32
        hbm = pl.BlockSpec(memory_space=pl.ANY)
        shown, before = pl.pallas_call(
            functools.partial(kernel, n, depths, rows, cols, length, nrec),
            out_shape=(
                jax.ShapeDtypeStruct((2, 2, rows + OFF, length), f32),
                jax.ShapeDtypeStruct((OFF, rows, length), f32),
            ),
            in_specs=[smem] * 5 + [hbm] + [vmem] * 4,
            out_specs=(hbm, hbm),
            scratch_shapes=[
                pltpu.VMEM((2, 2, rows, length), f32),
                pltpu.VMEM((OFF, rows, length), f32),
                pltpu.VMEM((4, length, length), jnp.bfloat16),
                pltpu.VMEM((2, 2, rows, length), f32),
                pltpu.VMEM((TICKS, 2, length, 2 * rows), f32),
                pltpu.VMEM((TICKS, 2, n, cols, 2 * rows), f32),
                pltpu.VMEM((TICKS, 2, length, 2 * cols), f32),
                pltpu.VMEM((TICKS, 2, n, rows, 2 * cols), f32),
                pltpu.VMEM((TICKS, 2, 2, rows + OFF, length), f32),
                pltpu.VMEM((TICKS, 2, cols, length), f32),
                pltpu.VMEM((TICKS, 2, rows, length), f32),
                pltpu.VMEM((8, 128), f32),
                pltpu.VMEM((8, 128), f32),
                pltpu.VMEM((2 * rows, length), f32),
                pltpu.SemaphoreType.DMA((TICKS, 2, 2, n)),
                pltpu.SemaphoreType.DMA((TICKS, 2, 2, n)),
                pltpu.SemaphoreType.DMA((2,)),
                pltpu.SemaphoreType.DMA((2,)),
                pltpu.SemaphoreType.DMA((TICKS, 2)),
                pltpu.SemaphoreType.DMA((TICKS, 2)),
                pltpu.SemaphoreType.DMA,
                pltpu.SemaphoreType.DMA,
                pltpu.SemaphoreType.DMA((2, 2)),
                pltpu.SemaphoreType.DMA,
                pltpu.SemaphoreType.DMA((2,)),
            ],
            compiler_params=pltpu.CompilerParams(
                collective_id=0, has_side_effects=True, vmem_limit_bytes=60 * 2**20
            ),
        )(
            slab_freq, ref_slow, inj_freq, wavelet[0], src_pos,
            waves.reshape(2, rows, 2, 1, length), table, slowness[0], rcv_pos.T, records[0, 0],
        )
        block = min(rows, 16)
        out, image = pl.pallas_call(
            functools.partial(finish, rows, length),
            grid=(rows // block,),
            out_shape=(
                jax.ShapeDtypeStruct((2, rows, 2, 1, length), f32),
                jax.ShapeDtypeStruct((OFF, rows, length), f32),
            ),
            in_specs=[
                pl.BlockSpec((2, 2, rows + OFF, length), lambda i: (0, 0, 0, 0)),
                pl.BlockSpec((OFF, block, length), lambda i: (0, i, 0)),
            ],
            out_specs=(hbm, pl.BlockSpec((OFF, block, length), lambda i: (0, i, 0))),
            scratch_shapes=[pltpu.SemaphoreType.DMA((2, 2))],
            compiler_params=pltpu.CompilerParams(vmem_limit_bytes=60 * 2**20),
        )(shown, before)
        return out.reshape(1, 2, rows, 2, 1, length), image[None]

    placed = (
        P(("shots", "depth"), None, "row", None, None, None),
        P(("shots", "depth"), None),
        P("depth", "row", None),
        P("depth"),
        P("shots", None),
        P("shots", None, None),
        P("shots", None, None, None),
        P("shots"),
        P("shots", None),
    )
    return jax.shard_map(
        local,
        mesh=mesh,
        in_specs=placed,
        out_specs=(
            P(("shots", "depth"), None, "row", None, None, None),
            P(("shots", "depth"), None, "row", None),
        ),
        check_vma=False,
    )
```

```python
import functools
import math

import jax
import jax.numpy as jnp
import numpy as np
from jax import lax
from jax.experimental import pallas as pl
from jax.experimental.pallas import tpu as pltpu
from jax.sharding import PartitionSpec as P

OFF = 16
TICKS = 2
DZ = 4

MESH = pl.DeviceIdType.MESH
NT = (((1,), (1,)), ((), ()))
NN = (((1,), (0,)), ((), ()))


def half_tables(length):
    half = length // 2
    a = np.arange(half)
    mats = []
    for odd in (0, 1):
        turn = ((2 * a[:, None] + odd) * a[None, :]) % length
        angle = turn * (2.0 * math.pi / length)
        c, s = np.cos(angle), np.sin(angle)
        mats.append(np.block([[c, s], [-s, c]]))
    stacked = []
    for m in (mats[0], mats[1]):
        high = m.astype(np.float32).astype(jnp.bfloat16)
        low = (m - high.astype(np.float64)).astype(np.float32).astype(jnp.bfloat16)
        stacked += [high, low]
    return np.stack(stacked)


def split(value):
    high = value.astype(jnp.bfloat16)
    low = (value - high.astype(jnp.float32)).astype(jnp.bfloat16)
    return high, low


def dot(a, b, dims):
    return lax.dot_general(a, b, dims, preferred_element_type=jnp.float32)


def table_first(high, low, data):
    d_high, d_low = split(data)
    return dot(high, d_high, NT) + (dot(high, d_low, NT) + dot(low, d_high, NT))


def data_first(data, high, low):
    d_high, d_low = split(data)
    return dot(d_high, high, NN) + (dot(d_low, high, NN) + dot(d_high, low, NN))


def cos_sin(angle):
    turns = jnp.floor(angle * (2.0 / math.pi) + 0.5)
    r = angle - turns * 1.5703125
    r = r - turns * 4.837512969970703125e-4
    r = r - turns * 7.54978995489188216e-8
    z = r * r
    sine = r + r * z * (-1.6666654611e-1 + z * (8.3321608736e-3 + z * -1.9515295891e-4))
    cosine = 1.0 - 0.5 * z + z * z * (
        4.166664568298827e-2 + z * (-1.388731625493765e-3 + z * 2.443315711809948e-5)
    )
    quarter = turns.astype(jnp.int32)
    swap = (quarter & 1) == 1
    c = jnp.where(swap, sine, cosine)
    s = jnp.where(swap, cosine, sine)
    c = jnp.where(((quarter + 1) & 2) == 2, -c, c)
    s = jnp.where((quarter & 2) == 2, -s, s)
    return c, s


def kernel(
    n, depths, rows, cols, length, nrec, parts,
    freq_ref, slow_ref, inj_ref, wavelet_ref, src_ref,
    waves_ref, table_ref, slowness_ref, pos_ref, rec_ref,
    shown_ref, image_out,
    u_first, image_ref, table_t, table_x, u_next, send1, recv1, send2, recv2, fld, phase, lens, freq_out, freq_in, hot,
    a2a_send, a2a_recv, z_send, z_recv, halo_send, halo_recv, f_send, f_recv, w_sem, i_sem, o_sem,
):
    half = length // 2
    wide = OFF // 2
    piece = rows // parts
    tiles = length // 128
    me = lax.axis_index("row")
    level = lax.axis_index("depth")
    deeper = level < depths - 1
    has_above = level > 0
    has_prev = me > 0
    has_next = me < n - 1

    def peer(off):
        return lax.rem(me + off, n)

    order = sorted(range(1, n), key=lambda off: abs(off - n / 2))

    def wave_copy(p, f):
        return pltpu.make_async_copy(waves_ref.at[p, :, f, 0, :], u_first.at[p, f], w_sem.at[p, f])

    def image_copy():
        return pltpu.make_async_copy(image_ref, image_out, i_sem)

    def shown_copy(f):
        return pltpu.make_async_copy(fld.at[TICKS - 1, :, f], shown_ref.at[:, f], o_sem.at[f])

    for f in (0, 1):
        for p in (0, 1):
            wave_copy(p, f).start()

    freq_out[...] = jnp.full(freq_out.shape, freq_ref[0, 0], jnp.float32)
    barrier = pltpu.get_barrier_semaphore()
    for off in order:
        pl.semaphore_signal(barrier, inc=1, device_id={"row": peer(off)}, device_id_type=MESH)

    @pl.when(deeper)
    def _():
        pl.semaphore_signal(barrier, inc=1, device_id={"depth": level + 1}, device_id_type=MESH)

    @pl.when(has_above)
    def _():
        pl.semaphore_signal(barrier, inc=1, device_id={"depth": level - 1}, device_id_type=MESH)

    sides = jnp.where(deeper, 1, 0) + jnp.where(has_above, 1, 0)
    pl.semaphore_wait(barrier, n - 1 + sides)

    below = lax.rem(level + 1, depths)

    def freq_copy():
        return pltpu.make_async_remote_copy(
            src_ref=freq_out, dst_ref=freq_in, send_sem=f_send, recv_sem=f_recv,
            device_id={"depth": below}, device_id_type=MESH)

    def z_copy(f, part):
        return pltpu.make_async_remote_copy(
            src_ref=fld.at[0, :, f, :, pl.ds(wide + part * piece, piece), :],
            dst_ref=u_next.at[:, f, :, pl.ds(part * piece, piece), :],
            send_sem=z_send.at[f, part], recv_sem=z_recv.at[f, part],
            device_id={"depth": below}, device_id_type=MESH)

    def a2a1_copy(t, f, part, off):
        to = peer(off)
        return pltpu.make_async_remote_copy(
            src_ref=send1.at[t, f, part, pl.ds(pl.multiple_of(to * cols, cols), cols), :],
            dst_ref=recv1.at[t, f, part, me],
            send_sem=a2a_send.at[t, 0, f, part, off], recv_sem=a2a_recv.at[t, 0, f, part, off],
            device_id={"row": to}, device_id_type=MESH)

    def a2a2_copy(t, f, part, off):
        to = peer(off)
        first = pl.multiple_of(to * rows + part * piece, piece)
        return pltpu.make_async_remote_copy(
            src_ref=send2.at[t, f, pl.ds(first, piece), :],
            dst_ref=recv2.at[t, f, me, pl.ds(part * piece, piece), :],
            send_sem=a2a_send.at[t, 1, f, part, off], recv_sem=a2a_recv.at[t, 1, f, part, off],
            device_id={"row": to}, device_id_type=MESH)

    def up_copy(t):
        return pltpu.make_async_remote_copy(
            src_ref=fld.at[t, :, :, :, pl.ds(rows, wide), :], dst_ref=fld.at[t, :, :, :, pl.ds(0, wide), :],
            send_sem=halo_send.at[t, 0], recv_sem=halo_recv.at[t, 0],
            device_id={"row": peer(1)}, device_id_type=MESH)

    def down_copy(t):
        return pltpu.make_async_remote_copy(
            src_ref=fld.at[t, :, :, :, pl.ds(wide, wide), :],
            dst_ref=fld.at[t, :, :, :, pl.ds(rows + wide, wide), :],
            send_sem=halo_send.at[t, 1], recv_sem=halo_recv.at[t, 1],
            device_id={"row": peer(n - 1)}, device_id_type=MESH)

    @pl.when(deeper)
    def _():
        freq_copy().start()

    def forward_y(t, f, part, real, imag):
        for parity in (0, 1):
            if parity == 0:
                folded = jnp.concatenate(
                    [real[:, :half] + real[:, half:], imag[:, :half] + imag[:, half:]], axis=1)
            else:
                folded = jnp.concatenate(
                    [real[:, :half] - real[:, half:], imag[:, :half] - imag[:, half:]], axis=1)
            result = table_first(table_ref[2 * parity], table_ref[2 * parity + 1], folded)
            send1[t, f, part, pl.ds(parity * half, half), pl.ds(0, piece)] = result[:half]
            send1[t, f, part, pl.ds(parity * half, half), pl.ds(piece, piece)] = result[half:]
        for off in order:
            a2a1_copy(t, f, part, off).start()
        recv1[t, f, part, me] = send1[t, f, part, pl.ds(pl.multiple_of(me * cols, cols), cols), :]

    def next_field(part):
        window = pl.ds(part * piece, piece)

        def read(f):
            return [
                jnp.concatenate([u_next[p, f, i, window, :] for i in range(tiles)], axis=1)
                for p in (0, 1)
            ]

        return read

    def forward_next(f, part):
        @pl.when(has_above)
        def _():
            z_copy(f, part).wait_recv()

        forward_y(1, f, part, *next_field(part)(f))

    def middle(t, f):
        for part in range(parts):
            for off in order:
                a2a1_copy(t, f, part, off).wait_recv()
        sign = 1.0 if f == 0 else -1.0
        pairs = [(s, part) for s in range(n // 2) for part in range(parts)]
        results = []
        for parity in (0, 1):
            pieces = []
            for s, part in pairs:
                near, far = recv1[t, f, part, s], recv1[t, f, part, s + n // 2]
                pieces.append(near + far if parity == 0 else near - far)
            folded = jnp.concatenate(pieces, axis=1)
            spectrum = data_first(folded, table_x[2 * parity], table_x[2 * parity + 1])
            p_real = phase[t, 0, :, pl.ds(parity * half, half)]
            p_imag = phase[t, 1, :, pl.ds(parity * half, half)] * sign
            s_real, s_imag = spectrum[:, :half], spectrum[:, half:]
            shifted = jnp.concatenate(
                [s_real * p_real - s_imag * p_imag, s_real * p_imag + s_imag * p_real], axis=1)
            results.append(table_first(table_t[2 * parity], table_t[2 * parity + 1], shifted))
        total = results[0] + results[1]
        send2[t, f, pl.ds(0, half), pl.ds(0, cols)] = total[:half]
        send2[t, f, pl.ds(0, half), pl.ds(cols, cols)] = total[half:]
        total = results[0] - results[1]
        send2[t, f, pl.ds(half, half), pl.ds(0, cols)] = total[:half]
        send2[t, f, pl.ds(half, half), pl.ds(cols, cols)] = total[half:]
        for part in range(parts):
            for off in order:
                a2a2_copy(t, f, part, off).start()
        recv2[t, f, me] = send2[t, f, pl.ds(pl.multiple_of(me * rows, rows), rows), :]

    def inverse_y(t, f, part):
        for off in order:
            a2a2_copy(t, f, part, off).wait_recv()
        sign = 1.0 if f == 0 else -1.0
        span = pl.ds(part * piece, piece)
        real = jnp.concatenate([recv2[t, f, s, span, pl.ds(0, cols)] for s in range(n)], axis=1)
        imag = jnp.concatenate([recv2[t, f, s, span, pl.ds(cols, cols)] for s in range(n)], axis=1)
        even = data_first(
            jnp.concatenate([real[:, :half], imag[:, :half]], axis=1), table_ref[0], table_ref[1])
        odd = data_first(
            jnp.concatenate([real[:, half:], imag[:, half:]], axis=1), table_ref[2], table_ref[3])
        for side in (0, 1):
            total = even + odd if side == 0 else even - odd
            window = pl.ds(side * half, half)
            l_cos = lens[t, 0, span, window]
            l_sin = lens[t, 1, span, window] * sign
            t_real, t_imag = total[:, :half], total[:, half:]
            new_real = t_real * l_cos - t_imag * l_sin
            new_imag = t_real * l_sin + t_imag * l_cos
            inner = pl.ds(wide + part * piece, piece)
            for i in range(half // 128):
                lanes = slice(i * 128, (i + 1) * 128)
                fld[t, 0, f, side * (half // 128) + i, inner, :] = new_real[:, lanes]
                fld[t, 1, f, side * (half // 128) + i, inner, :] = new_imag[:, lanes]

    def wave_number(index):
        order_of = jnp.where(index < half, 2 * index, 2 * (index - half) + 1)
        signed = jnp.where(order_of < half, order_of, order_of - length)
        k = signed.astype(jnp.float32) * (2.0 * math.pi / length)
        return k * k

    def factors(t, freq):
        ref_slow = slow_ref[0]
        number = freq * ref_slow
        block = min(cols, 32)

        def phase_block(i, carry):
            base = pl.multiple_of(i * block, block)
            ky = wave_number(lax.broadcasted_iota(jnp.int32, (block, length), 0) + (me * cols + base))
            kx = wave_number(lax.broadcasted_iota(jnp.int32, (block, length), 1))
            vertical = number * number - (kx + ky)
            root = jnp.sqrt(jnp.abs(vertical)) * float(DZ)
            moving = vertical > 0
            c, s = cos_sin(root)
            scale = 1.0 / (length * length)
            phase[t, 0, pl.ds(base, block), :] = jnp.where(moving, c, jnp.exp(-root)) * scale
            phase[t, 1, pl.ds(base, block), :] = jnp.where(moving, s, 0.0) * scale
            return carry

        lax.fori_loop(0, cols // block, phase_block, 0)
        block_r = min(rows, 32)

        def lens_block(i, carry):
            base = pl.multiple_of(i * block_r, block_r)
            angle = freq * (slowness_ref[pl.ds(base, block_r), :] - ref_slow) * float(DZ)
            c, s = cos_sin(angle)
            lens[t, 0, pl.ds(base, block_r), :] = c
            lens[t, 1, pl.ds(base, block_r), :] = s
            return carry

        lax.fori_loop(0, rows // block_r, lens_block, 0)

    def inject():
        row_ids = lax.broadcasted_iota(jnp.int32, (rows, 1), 0) + me * rows
        col_ids = lax.broadcasted_iota(jnp.int32, (1, length), 1)
        point = (row_ids == src_ref[0]) & (col_ids == src_ref[1])
        for p in (0, 1):
            source = jnp.where(point, wavelet_ref[0, p], 0.0)
            for i in range(tiles):
                u_next[p, 0, i] = source[:, i * 128:(i + 1) * 128]
        chunk = min(512, nrec)

        def step(i, carry):
            base = pl.multiple_of(i * chunk, chunk)
            x = pos_ref[pl.ds(0, 1), pl.ds(base, chunk)]
            y = pos_ref[pl.ds(1, 1), pl.ds(base, chunk)]
            in_row = lax.broadcasted_iota(jnp.int32, (rows, chunk), 0) + me * rows == x
            in_col = jnp.where(
                lax.broadcasted_iota(jnp.int32, (length, chunk), 0) == y, 1.0, 0.0).astype(jnp.bfloat16)
            both = []
            for p in (0, 1):
                value = rec_ref[pl.ds(p, 1), pl.ds(base, chunk)]
                both.append(jnp.where(in_row, value, 0.0))
            left = jnp.concatenate(both, axis=0)
            high, low = split(left)
            added = dot(high, in_col, NT) + dot(low, in_col, NT)
            hot[...] = hot[...] + added
            return carry

        hot[...] = jnp.zeros_like(hot)
        lax.fori_loop(0, nrec // chunk, step, 0)
        for p in (0, 1):
            for i in range(tiles):
                u_next[p, 1, i] = hot[pl.ds(p * rows, rows), pl.ds(i * 128, 128)]

    def halo_start(t):
        zero = jnp.zeros((2, 2, tiles, wide, 128), jnp.float32)

        @pl.when(has_next)
        def _():
            up_copy(t).start()

        @pl.when(has_prev)
        def _():
            down_copy(t).start()

        @pl.when(jnp.logical_not(has_prev))
        def _():
            fld[t, :, :, :, pl.ds(0, wide), :] = zero

        @pl.when(jnp.logical_not(has_next))
        def _():
            fld[t, :, :, :, pl.ds(rows + wide, wide), :] = zero

    def halo_wait(t):
        @pl.when(has_prev)
        def _():
            up_copy(t).wait_recv()

        @pl.when(has_next)
        def _():
            down_copy(t).wait_recv()

    def imaging(t):
        def block(i, carry):
            base = pl.multiple_of(i * 8, 8)
            for i_tile in range(tiles):
                for j in range(OFF):
                    h = j - wide
                    behind, ahead = pl.ds(base + (wide - h), 8), pl.ds(base + (wide + h), 8)
                    image_ref[j, pl.ds(base, 8), pl.ds(i_tile * 128, 128)] = (
                        fld[t, 0, 0, i_tile, behind, :] * fld[t, 0, 1, i_tile, ahead, :]
                        + fld[t, 1, 0, i_tile, behind, :] * fld[t, 1, 1, i_tile, ahead, :])
            return carry

        lax.fori_loop(0, rows // 8, block, 0)

    for f in (0, 1):
        for p in (0, 1):
            wave_copy(p, f).wait()
        for part in range(parts):
            window = pl.ds(part * piece, piece)
            forward_y(0, f, part, u_first[0, f, window, :], u_first[1, f, window, :])
    for i in range(4):
        flipped = table_ref[i].T
        table_t[i] = flipped
        place = 0
        for s in range(n // 2):
            for part in range(parts):
                for p in (0, 1):
                    first = p * half + s * rows + part * piece
                    table_x[i, pl.ds(place, piece), :] = flipped[first:first + piece]
                    place += piece
    factors(0, freq_ref[0, 0])
    middle(0, 0)

    @pl.when(jnp.logical_not(has_above))
    def _():
        factors(1, inj_ref[0, 0])

    @pl.when(has_above)
    def _():
        freq_copy().wait_recv()
        factors(1, freq_in[pl.ds(0, 1), pl.ds(0, 1)])

    middle(0, 1)
    for f in (0, 1):
        for part in range(parts):
            inverse_y(0, f, part)

            @pl.when(deeper)
            def _():
                z_copy(f, part).start()

    halo_start(0)

    @pl.when(jnp.logical_not(has_above))
    def _():
        inject()

    for part in range(parts):
        forward_next(0, part)
    halo_wait(0)
    imaging(0)
    image_copy().start()
    middle(1, 0)
    for part in range(parts):
        forward_next(1, part)
    middle(1, 1)
    for f in (0, 1):
        for part in range(parts):
            inverse_y(1, f, part)
    halo_start(1)
    halo_wait(1)
    for f in (0, 1):
        shown_copy(f).start()

    for t in range(TICKS):
        for f in (0, 1):
            for part in range(parts):
                for off in order:
                    a2a1_copy(t, f, part, off).wait_send()
                    a2a2_copy(t, f, part, off).wait_send()

        @pl.when(has_next)
        def _():
            up_copy(t).wait_send()

        @pl.when(has_prev)
        def _():
            down_copy(t).wait_send()

    @pl.when(deeper)
    def _():
        freq_copy().wait_send()
        for f in (0, 1):
            for part in range(parts):
                z_copy(f, part).wait_send()

    image_copy().wait()
    for f in (0, 1):
        shown_copy(f).wait()


def finish(rows, length, fld_ref, before_ref, out_ref, image_ref, o_sem):
    wide = OFF // 2
    tiles = length // 128
    step = pl.program_id(0)
    block = image_ref.shape[1]

    def out_copy(p, f):
        return [
            pltpu.make_async_copy(
                fld_ref.at[p, f, i, pl.ds(wide, rows), :],
                out_ref.at[p, :, f, 0, pl.ds(i * 128, 128)], o_sem.at[p, f, i])
            for i in range(tiles)
        ]

    @pl.when(step == 0)
    def _():
        for f in (0, 1):
            for p in (0, 1):
                for copy in out_copy(p, f):
                    copy.start()

    def part(i, carry):
        base = pl.multiple_of(i * 8, 8)
        top = step * block + base
        for i_tile in range(tiles):
            lanes = pl.ds(i_tile * 128, 128)
            for j in range(OFF):
                h = j - wide
                behind, ahead = pl.ds(top + (wide - h), 8), pl.ds(top + (wide + h), 8)
                term = (
                    fld_ref[0, 0, i_tile, behind, :] * fld_ref[0, 1, i_tile, ahead, :]
                    + fld_ref[1, 0, i_tile, behind, :] * fld_ref[1, 1, i_tile, ahead, :])
                image_ref[j, pl.ds(base, 8), lanes] = before_ref[j, pl.ds(base, 8), lanes] + term
        return carry

    lax.fori_loop(0, block // 8, part, 0)

    @pl.when(step == pl.num_programs(0) - 1)
    def _():
        for f in (0, 1):
            for p in (0, 1):
                for copy in out_copy(p, f):
                    copy.wait()


def solution(mesh):
    n, depths = mesh.shape["row"], mesh.shape["depth"]

    def local(waves, slab_freq, slowness, ref_slow, inj_freq, wavelet, records, src_pos, rcv_pos):
        rows, length = waves.shape[2], waves.shape[5]
        cols = length // n
        nrec = rcv_pos.shape[0]
        assert waves.shape[4] == 1 and slowness.shape[0] == 1
        assert inj_freq.shape[0] == TICKS - 1
        table = jnp.asarray(half_tables(length), jnp.bfloat16)
        vmem = pl.BlockSpec(memory_space=pltpu.VMEM)
        smem = pl.BlockSpec(memory_space=pltpu.SMEM)
        f32 = jnp.float32
        parts = 2 if rows >= 128 else 1
        tiles = length // 128
        hbm = pl.BlockSpec(memory_space=pl.ANY)
        shown, before = pl.pallas_call(
            functools.partial(kernel, n, depths, rows, cols, length, nrec, parts),
            out_shape=(
                jax.ShapeDtypeStruct((2, 2, tiles, rows + OFF, 128), f32),
                jax.ShapeDtypeStruct((OFF, rows, length), f32),
            ),
            in_specs=[smem] * 5 + [hbm] + [vmem] * 4,
            out_specs=(hbm, hbm),
            scratch_shapes=[
                pltpu.VMEM((2, 2, rows, length), f32),
                pltpu.VMEM((OFF, rows, length), f32),
                pltpu.VMEM((4, length, length), jnp.bfloat16),
                pltpu.VMEM((4, length, length), jnp.bfloat16),
                pltpu.VMEM((2, 2, tiles, rows, 128), f32),
                pltpu.VMEM((TICKS, 2, parts, length, 2 * rows // parts), f32),
                pltpu.VMEM((TICKS, 2, parts, n, cols, 2 * rows // parts), f32),
                pltpu.VMEM((TICKS, 2, length, 2 * cols), f32),
                pltpu.VMEM((TICKS, 2, n, rows, 2 * cols), f32),
                pltpu.VMEM((TICKS, 2, 2, tiles, rows + OFF, 128), f32),
                pltpu.VMEM((TICKS, 2, cols, length), f32),
                pltpu.VMEM((TICKS, 2, rows, length), f32),
                pltpu.VMEM((8, 128), f32),
                pltpu.VMEM((8, 128), f32),
                pltpu.VMEM((2 * rows, length), f32),
                pltpu.SemaphoreType.DMA((TICKS, 2, 2, parts, n)),
                pltpu.SemaphoreType.DMA((TICKS, 2, 2, parts, n)),
                pltpu.SemaphoreType.DMA((2, parts)),
                pltpu.SemaphoreType.DMA((2, parts)),
                pltpu.SemaphoreType.DMA((TICKS, 2)),
                pltpu.SemaphoreType.DMA((TICKS, 2)),
                pltpu.SemaphoreType.DMA,
                pltpu.SemaphoreType.DMA,
                pltpu.SemaphoreType.DMA((2, 2)),
                pltpu.SemaphoreType.DMA,
                pltpu.SemaphoreType.DMA((2,)),
            ],
            compiler_params=pltpu.CompilerParams(
                collective_id=0, has_side_effects=True, vmem_limit_bytes=60 * 2**20
            ),
        )(
            slab_freq, ref_slow, inj_freq, wavelet[0], src_pos,
            waves.reshape(2, rows, 2, 1, length), table, slowness[0], rcv_pos.T, records[0, 0],
        )
        block = min(rows, 16)
        out, image = pl.pallas_call(
            functools.partial(finish, rows, length),
            grid=(rows // block,),
            out_shape=(
                jax.ShapeDtypeStruct((2, rows, 2, 1, length), f32),
                jax.ShapeDtypeStruct((OFF, rows, length), f32),
            ),
            in_specs=[
                pl.BlockSpec((2, 2, tiles, rows + OFF, 128), lambda i: (0, 0, 0, 0, 0)),
                pl.BlockSpec((OFF, block, length), lambda i: (0, i, 0)),
            ],
            out_specs=(hbm, pl.BlockSpec((OFF, block, length), lambda i: (0, i, 0))),
            scratch_shapes=[pltpu.SemaphoreType.DMA((2, 2, tiles))],
            compiler_params=pltpu.CompilerParams(vmem_limit_bytes=60 * 2**20),
        )(shown, before)
        return out.reshape(1, 2, rows, 2, 1, length), image[None]

    placed = (
        P(("shots", "depth"), None, "row", None, None, None),
        P(("shots", "depth"), None),
        P("depth", "row", None),
        P("depth"),
        P("shots", None),
        P("shots", None, None),
        P("shots", None, None, None),
        P("shots"),
        P("shots", None),
    )
    return jax.shard_map(
        local,
        mesh=mesh,
        in_specs=placed,
        out_specs=(
            P(("shots", "depth"), None, "row", None, None, None),
            P(("shots", "depth"), None, "row", None),
        ),
        check_vma=False,
    )
```
